32 devices in a mesh: grp: 2 (over x), beam: 16 (over z, y, core).
Axes of the slice: x: 2, y: 2, z: 4, core: 2. Of those that a mesh axis runs over, the one named last changes fastest.
Arguments:
- s_matrix: bfloat16 [2, 2048, 16, 4096], P(None, ('grp', 'beam')), parts along dimension 1, may hold values from -6 to 6
- beam_weight: float32 [2, 2048], P(None, ('grp', 'beam')), parts along dimension 1, may hold values from -0.25 to 0.25
- probe_shift: int32 [256, 2], P(('grp', 'beam')), parts along dimension 0, may hold values from 0 to 191
- probe_cutoff: int32 [256], P(('grp', 'beam')), parts along dimension 0, may hold values from 64 to 512
- target: bfloat16 [2, 256, 4096], P(None, ('grp', 'beam')), parts along dimension 1, may hold values from -3 to 3
- target_exp: int32 [256], P(('grp', 'beam')), parts along dimension 0, may hold values from -1 to 2
Outputs:
- s_grad: bfloat16 [2, 2048, 16, 4096], P(None, ('grp', 'beam')), parts along dimension 1
The draws below stay inside these ranges and needn't reach their ends.
There are 2 independent parts, one for each index of `grp`. The reference program is written for one: setup_inputs(seed, part) draws one part's arguments, and reference() takes and returns one part's arrays. A program takes and returns all parts, laid end to end along the dimension named above; each array names one. Nothing has to cross between parts.
All inputs are finite; a program needn't handle non-finite values.
Results may differ from the reference program's by a relative error of at most 0.006.
Values may be sent and summed in bfloat16 or wider, within the bound.
A program may use at most 128 MiB of HBM per device.

```python
import math
import jax
import jax.numpy as jnp
from jax import lax

SIDE = 32
BEAMS = 1024
PIX = 4096
GRID = 192
TILE_SIDE = 4
TILES = 16
PROBES = 128


def set_ends(array, own_key, smallest, top_value):
    extent = array.shape
    spot = [jax.random.randint(jax.random.fold_in(own_key, axis), (), 0, extent[axis]) for axis in range(len(extent))]
    array = array.at[tuple(spot)].set(smallest)
    longest = extent.index(max(extent))
    spot[longest] = (spot[longest] + 1) % extent[longest]
    return array.at[tuple(spot)].set(top_value)


def levels(stream_key, dims, split, smallest, top_value):
    loudness, own = 1.0, jax.random.fold_in(stream_key, 6)
    for axis_at, blocks in split:
        heights = jnp.exp(jax.random.uniform(jax.random.fold_in(own, axis_at), (blocks,), jnp.float32, smallest / len(split), top_value / len(split)))
        loudness = loudness * jnp.repeat(heights, dims[axis_at] // blocks).reshape([-1 if axis == axis_at else 1 for axis in range(len(dims))])
    return loudness


def bell_draw(own_key, shape, spread, most, split=(), kind=jnp.bfloat16):
    array = jax.random.normal(own_key, shape, jnp.float32) * spread
    if len(split) > 0:
        array = levels(own_key, shape, split, -0.22, 0.18) * array
    return jnp.clip(array, min=-most, max=most).astype(kind)


def setup_inputs(seed: int = 0, part: int = 0) -> dict:
    streams_of = jax.random.split(jax.random.key(seed), 7)
    own_keys = jax.random.split(jax.random.fold_in(streams_of[6], part), 7)
    s_matrix = bell_draw(own_keys[0], (2, BEAMS, TILES, PIX), 1.0, 6.0, ((1, 16),))
    beam_weight = bell_draw(own_keys[1], (2, BEAMS), (BEAMS // 2) ** -0.5, 0.25, ((1, 16),), jnp.float32)
    probe_shift = set_ends(jax.random.randint(own_keys[2], (PROBES, 2), 0, GRID), jax.random.fold_in(own_keys[2], 1), 0, GRID - 1).astype(jnp.int32)
    probe_cutoff = set_ends(jax.random.randint(own_keys[3], (PROBES,), BEAMS // 16, BEAMS // 2 + 1), jax.random.fold_in(own_keys[3], 1), BEAMS // 16, (BEAMS // 2 + 1) - 1).astype(jnp.int32)
    target = bell_draw(own_keys[4], (2, PROBES, PIX), 0.5, 3.0, ((1, 16),))
    target_exp = set_ends(jax.random.randint(own_keys[5], (PROBES,), -1, 3), jax.random.fold_in(own_keys[5], 1), -1, 2).astype(jnp.int32)
    return dict(s_matrix=s_matrix, beam_weight=beam_weight, probe_shift=probe_shift, probe_cutoff=probe_cutoff, target=target, target_exp=target_exp)


TWO_PI = 2.0 * math.pi

def window_of(shift):
    step = GRID // TILE_SIDE
    return shift[:, 0] // step * TILE_SIDE + shift[:, 1] // step

def coefficients(beam_index, weight, shift, cutoff):
    half = SIDE // 2
    freq_x = beam_index % SIDE - half
    freq_y = beam_index // SIDE - half
    ramp = (freq_x[None, :] * shift[:, 0:1] + freq_y[None, :] * shift[:, 1:2]) % GRID
    phase = ramp.astype(jnp.float32) * (TWO_PI / GRID)
    inside = (freq_x * freq_x + freq_y * freq_y)[None, :] <= cutoff[:, None]
    cosine = jnp.cos(phase)
    sine = jnp.sin(phase)
    w_real = weight[0][None, :]
    w_imag = weight[1][None, :]
    c_real = jnp.where(inside, w_real * cosine + w_imag * sine, 0.0)
    c_imag = jnp.where(inside, w_imag * cosine - w_real * sine, 0.0)
    return (c_real.astype(jnp.bfloat16), c_imag.astype(jnp.bfloat16))

def reference(s_matrix, beam_weight, probe_shift, probe_cutoff, target, target_exp):
    group = 32
    count = BEAMS // group
    s_blocks = s_matrix.reshape(2, count, group, TILES, PIX).transpose(1, 0, 2, 3, 4)
    w_blocks = beam_weight.reshape(2, count, group).transpose(1, 0, 2)
    starts = jnp.arange(count, dtype=jnp.int32) * group
    windows = window_of(probe_shift)
    onehot = windows[:, None] == jnp.arange(TILES, dtype=jnp.int32)[None, :]

    def expand(start, weight):
        index = start + jnp.arange(group, dtype=jnp.int32)
        c_real, c_imag = coefficients(index, weight, probe_shift, probe_cutoff)
        zero = jnp.zeros((), jnp.bfloat16)
        e_real = jnp.where(onehot[:, None, :], c_real[:, :, None], zero).reshape(PROBES, group * TILES)
        e_imag = jnp.where(onehot[:, None, :], c_imag[:, :, None], zero).reshape(PROBES, group * TILES)
        return (e_real, e_imag)

    def add_wave(total, item):
        start, block, weight = item
        e_real, e_imag = expand(start, weight)
        s_re = block[0].reshape(group * TILES, PIX)
        s_im = block[1].reshape(group * TILES, PIX)
        w_re = jnp.dot(e_real, s_re, preferred_element_type=jnp.float32) - jnp.dot(e_imag, s_im, preferred_element_type=jnp.float32)
        w_im = jnp.dot(e_real, s_im, preferred_element_type=jnp.float32) + jnp.dot(e_imag, s_re, preferred_element_type=jnp.float32)
        return ((total[0] + w_re, total[1] + w_im), None)
    empty = jnp.zeros((PROBES, PIX), jnp.float32)
    (wave_re, wave_im), _ = lax.scan(add_wave, (empty, empty), (starts, s_blocks, w_blocks))
    scale = jnp.exp2(target_exp.astype(jnp.float32))[None, :, None]
    scaled = target.astype(jnp.float32) * scale
    residual = (jnp.stack([wave_re, wave_im]) - scaled).astype(jnp.bfloat16)

    def grad(item):
        start, weight = item
        e_real, e_imag = expand(start, weight)
        g_re = jnp.dot(e_real.T, residual[0], preferred_element_type=jnp.float32) + jnp.dot(e_imag.T, residual[1], preferred_element_type=jnp.float32)
        g_im = jnp.dot(e_real.T, residual[1], preferred_element_type=jnp.float32) - jnp.dot(e_imag.T, residual[0], preferred_element_type=jnp.float32)
        return jnp.stack([g_re, g_im]).reshape(2, group, TILES, PIX).astype(jnp.bfloat16)
    blocks = lax.map(grad, (starts, w_blocks))
    return blocks.transpose(1, 0, 2, 3, 4).reshape(2, BEAMS, TILES, PIX)
```

```python
import functools
import math

import jax
import jax.numpy as jnp
from jax import lax
from jax.experimental import pallas as pl
from jax.experimental.pallas import tpu as pltpu
from jax.sharding import PartitionSpec as P

SIDE = 32
GRID = 192
TILE_SIDE = 4
TWO_PI = 2.0 * math.pi
CHUNKS = 4
MATMUL_COLUMNS = 512


def stage_strides(n):
    return [2**k for k in range(n.bit_length() - 1)]


def place(me, strides, unit, upto):
    levels = len(strides)
    base = 0
    for k in range(upto):
        base = base + (me // strides[k]) % 2 * (unit * 2 ** (levels - 1 - k))
    return base


def wave_kernel(
    n, local, tile_count, pixels, strides,
    par_ref, weight_ref, target_ref, s_ref,
    res_ref, left_ref,
    pars, s_vmem, acc, sbuf, rbuf,
    par_send, par_recv, s_sem, send_sem, recv_sem,
):
    levels = len(strides)
    me = lax.axis_index("beam")
    unit = par_ref.shape[0]
    rows = n * unit
    width = local * tile_count
    wide = pixels // CHUNKS

    def partner(k):
        return me + (1 - 2 * ((me // strides[k]) % 2)) * strides[k]

    def columns(c):
        return pl.ds(c * wide, wide)

    loads = []
    for c in range(CHUNKS):
        load = pltpu.make_async_copy(s_ref.at[:, columns(c)], s_vmem.at[:, columns(c)], s_sem.at[c])
        load.start()
        loads.append(load)

    barrier = pltpu.get_barrier_semaphore()
    for k in range(levels):
        pl.semaphore_signal(barrier, inc=1, device_id={"beam": partner(k)}, device_id_type=pl.DeviceIdType.MESH)
    pl.semaphore_wait(barrier, levels)

    sent = []

    def send(source, target, send_semaphore, recv_semaphore, k):
        copy = pltpu.make_async_remote_copy(
            src_ref=source,
            dst_ref=target,
            send_sem=send_semaphore,
            recv_sem=recv_semaphore,
            device_id={"beam": partner(k)},
            device_id_type=pl.DeviceIdType.MESH,
        )
        copy.start()
        sent.append(copy)
        return copy

    def mine(k):
        size = unit * 2 ** (levels - k)
        return pl.ds(pl.multiple_of(place(me, strides, unit, k), size), size)

    pars[mine(levels), :] = par_ref[...]
    for k in reversed(range(levels)):
        held = pars.at[mine(k + 1), :]
        send(held, held, par_send.at[k], par_recv.at[k], k).wait_recv()

    half = SIDE // 2
    beam = me * local + lax.broadcasted_iota(jnp.int32, (1, local), 1)
    freq_x = beam % SIDE - half
    freq_y = beam // SIDE - half
    shift_x = pars[:, 0:1]
    shift_y = pars[:, 1:2]
    cutoff = pars[:, 2:3]
    ramp = (freq_x * shift_x + freq_y * shift_y) % GRID
    phase = ramp.astype(jnp.float32) * (TWO_PI / GRID)
    inside = (freq_x * freq_x + freq_y * freq_y) <= cutoff
    cosine = jnp.cos(phase)
    sine = jnp.sin(phase)
    w_real = weight_ref[0:1, :]
    w_imag = weight_ref[1:2, :]
    c_real = jnp.where(inside, w_real * cosine + w_imag * sine, 0.0)
    c_imag = jnp.where(inside, w_imag * cosine - w_real * sine, 0.0)
    is_real = lax.broadcasted_iota(jnp.int32, (rows, 1), 0) % unit < unit // 2
    first = jnp.where(is_real, c_real, c_imag).astype(jnp.bfloat16)
    second = jnp.where(is_real, -c_imag, c_real).astype(jnp.bfloat16)
    step = GRID // TILE_SIDE
    window = shift_x // step * TILE_SIDE + shift_y // step
    place_of = lax.broadcasted_iota(jnp.int32, (1, width), 1)
    chosen = window == place_of % tile_count
    spread = lax.broadcasted_iota(jnp.int32, (local, width), 1) // tile_count
    spread = (spread == lax.broadcasted_iota(jnp.int32, (local, width), 0)).astype(jnp.float32).astype(jnp.bfloat16)
    for at, part in ((0, first), (width, second)):
        full = jnp.dot(part, spread, preferred_element_type=jnp.float32)
        left_ref[:, at : at + width] = jnp.where(chosen, full, 0.0).astype(jnp.bfloat16)

    narrow = min(MATMUL_COLUMNS, wide)

    def multiply(c):
        def tile(i, carry):
            at = pl.ds(pl.multiple_of(c * wide + i * narrow, narrow), narrow)
            acc[:, at] = jnp.dot(left_ref[...], s_vmem[:, at], preferred_element_type=jnp.float32)
            return carry

        lax.fori_loop(0, wide // narrow, tile, 0)

    def scatter_rows(k):
        size = rows // 2 ** (k + 1)
        base = place(me, strides, unit, k)
        bit = (me // strides[k]) % 2
        keep = pl.ds(pl.multiple_of(base + bit * size, size), size)
        give = pl.ds(pl.multiple_of(base + (1 - bit) * size, size), size)
        slot = pl.ds(rows - 2 * size, size)
        return keep, give, slot

    def start_scatter(c, k):
        _, give, slot = scatter_rows(k)
        sbuf[slot, columns(c)] = acc[give, columns(c)].astype(jnp.bfloat16)
        return send(
            sbuf.at[slot, columns(c)], rbuf.at[slot, columns(c)], send_sem.at[c, k], recv_sem.at[c, k], k
        )

    def end_scatter(c, k):
        keep, _, slot = scatter_rows(k)
        acc[keep, columns(c)] += rbuf[slot, columns(c)].astype(jnp.float32)

    def residual(c):
        own = mine(levels)
        scale = jnp.exp2(par_ref[:, 3:4].astype(jnp.float32))
        goal = target_ref[:, columns(c)].astype(jnp.float32) * scale
        res_ref[own, columns(c)] = (acc[own, columns(c)] - goal).astype(jnp.bfloat16)

    def start_gather(c, k):
        held = res_ref.at[mine(k + 1), columns(c)]
        at = 2 * levels - 1 - k
        return send(held, held, send_sem.at[c, at], recv_sem.at[c, at], k)

    flight = {}
    for time in range(CHUNKS + 2 * levels):
        for c in range(CHUNKS):
            at = time - c
            if at < 0 or at > 2 * levels:
                continue
            if at == 0:
                loads[c].wait()
                multiply(c)
            else:
                flight[c].wait_recv()
                if at <= levels:
                    end_scatter(c, at - 1)
            if at < levels:
                flight[c] = start_scatter(c, at)
            elif at < 2 * levels:
                if at == levels:
                    residual(c)
                flight[c] = start_gather(c, 2 * levels - 1 - at)
    for copy in sent:
        copy.wait_send()


def body(n, s_matrix, beam_weight, probe_shift, probe_cutoff, target, target_exp):
    _, local, tile_count, pixels = s_matrix.shape
    probes = probe_shift.shape[0]
    strides = stage_strides(n)
    levels = len(strides)
    unit = 2 * probes
    rows = n * unit
    width = local * tile_count
    pars = jnp.concatenate([probe_shift, probe_cutoff[:, None], target_exp[:, None]], axis=1)
    pars = jnp.pad(jnp.concatenate([pars, pars], axis=0), ((0, 0), (0, 124)))
    vmem = pl.BlockSpec(memory_space=pltpu.VMEM)
    res, left = pl.pallas_call(
        functools.partial(wave_kernel, n, local, tile_count, pixels, strides),
        out_shape=(
            jax.ShapeDtypeStruct((rows, pixels), jnp.bfloat16),
            jax.ShapeDtypeStruct((rows, 2 * width), jnp.bfloat16),
        ),
        in_specs=[vmem, vmem, vmem, pl.BlockSpec(memory_space=pl.ANY)],
        out_specs=(vmem, vmem),
        scratch_shapes=[
            pltpu.VMEM((rows, 128), jnp.int32),
            pltpu.VMEM((2 * width, pixels), jnp.bfloat16),
            pltpu.VMEM((rows, pixels), jnp.float32),
            pltpu.VMEM((rows, pixels), jnp.bfloat16),
            pltpu.VMEM((rows, pixels), jnp.bfloat16),
            pltpu.SemaphoreType.DMA((levels,)),
            pltpu.SemaphoreType.DMA((levels,)),
            pltpu.SemaphoreType.DMA((CHUNKS,)),
            pltpu.SemaphoreType.DMA((CHUNKS, 2 * levels)),
            pltpu.SemaphoreType.DMA((CHUNKS, 2 * levels)),
        ],
        compiler_params=pltpu.CompilerParams(
            collective_id=0, has_side_effects=True, vmem_limit_bytes=60 * 2**20
        ),
    )(pars, beam_weight, target.reshape(unit, pixels), s_matrix.reshape(2 * width, pixels))
    grad = lax.dot_general(left, res, (((0,), (0,)), ((), ())), preferred_element_type=jnp.float32)
    return grad.astype(jnp.bfloat16).reshape(2, local, tile_count, pixels)


def solution(mesh):
    return jax.shard_map(
        functools.partial(body, mesh.shape["beam"]),
        mesh=mesh,
        in_specs=(
            P(None, ("grp", "beam"), None, None),
            P(None, ("grp", "beam")),
            P(("grp", "beam"), None),
            P(("grp", "beam")),
            P(None, ("grp", "beam"), None),
            P(("grp", "beam")),
        ),
        out_specs=P(None, ("grp", "beam"), None, None),
        check_vma=False,
    )
```

```python
import functools
import math

import jax
import jax.numpy as jnp
from jax import lax
from jax.experimental import pallas as pl
from jax.experimental.pallas import tpu as pltpu
from jax.sharding import PartitionSpec as P

SIDE = 32
GRID = 192
TILE_SIDE = 4
TWO_PI = 2.0 * math.pi
CHUNKS = 8
SWAP = False
GAP_NEAR = 2
GAP_FAR = 3
MATMUL_COLUMNS = 512


def stage_strides(n):
    return [2**k for k in range(n.bit_length() - 1)]


def orders(n):
    strides = stage_strides(n)
    other = list(strides)
    if SWAP and len(other) > 2:
        other[1], other[2] = other[2], other[1]
    return strides, other


def place(me, strides, unit, upto):
    levels = len(strides)
    base = 0
    for k in range(upto):
        base = base + (me // strides[k]) % 2 * (unit * 2 ** (levels - 1 - k))
    return base


def wave_kernel(
    n, local, tile_count, pixels, strides, other,
    par_ref, weight_ref, target_ref, s_ref,
    res_ref, left_ref,
    pars, s_vmem, acc, sbuf, rbuf, mixed_left, mixed_res,
    par_send, par_recv, s_sem, send_sem, recv_sem,
):
    levels = len(strides)
    me = lax.axis_index("beam")
    unit = par_ref.shape[0]
    rows = n * unit
    width = local * tile_count
    wide = pixels // CHUNKS

    def order(c):
        return other if c % 2 else strides

    moves = [(place(i, other, unit, levels), place(i, strides, unit, levels)) for i in range(n)]

    def partner(stride):
        return me + (1 - 2 * ((me // stride) % 2)) * stride

    def columns(c):
        return pl.ds(c * wide, wide)

    loads = []
    for c in range(CHUNKS):
        load = pltpu.make_async_copy(s_ref.at[:, columns(c)], s_vmem.at[:, columns(c)], s_sem.at[c])
        load.start()
        loads.append(load)

    barrier = pltpu.get_barrier_semaphore()
    for ahead in range(1, n):
        pl.semaphore_signal(
            barrier, inc=1, device_id={"beam": lax.rem(me + ahead, n)}, device_id_type=pl.DeviceIdType.MESH
        )
    pl.semaphore_wait(barrier, n - 1)

    sent = []

    def send(source, target, send_semaphore, recv_semaphore, peer):
        copy = pltpu.make_async_remote_copy(
            src_ref=source,
            dst_ref=target,
            send_sem=send_semaphore,
            recv_sem=recv_semaphore,
            device_id={"beam": peer},
            device_id_type=pl.DeviceIdType.MESH,
        )
        copy.start()
        sent.append(copy)
        return copy

    def mine(k, steps=strides):
        size = unit * 2 ** (levels - k)
        return pl.ds(pl.multiple_of(place(me, steps, unit, k), size), size)

    pars[mine(levels), :] = par_ref[...]
    asked = [
        send(par_ref, pars.at[mine(levels), :], par_send.at[ahead - 1], par_recv.at[ahead - 1], lax.rem(me + ahead, n))
        for ahead in range(1, n)
    ]
    for copy in asked:
        copy.wait_recv()

    half = SIDE // 2
    beam = me * local + lax.broadcasted_iota(jnp.int32, (1, local), 1)
    freq_x = beam % SIDE - half
    freq_y = beam // SIDE - half
    shift_x = pars[:, 0:1]
    shift_y = pars[:, 1:2]
    cutoff = pars[:, 2:3]
    ramp = (freq_x * shift_x + freq_y * shift_y) % GRID
    phase = ramp.astype(jnp.float32) * (TWO_PI / GRID)
    inside = (freq_x * freq_x + freq_y * freq_y) <= cutoff
    cosine = jnp.cos(phase)
    sine = jnp.sin(phase)
    w_real = weight_ref[0:1, :]
    w_imag = weight_ref[1:2, :]
    c_real = jnp.where(inside, w_real * cosine + w_imag * sine, 0.0)
    c_imag = jnp.where(inside, w_imag * cosine - w_real * sine, 0.0)
    is_real = lax.broadcasted_iota(jnp.int32, (rows, 1), 0) % unit < unit // 2
    first = jnp.where(is_real, c_real, c_imag).astype(jnp.bfloat16)
    second = jnp.where(is_real, -c_imag, c_real).astype(jnp.bfloat16)
    step = GRID // TILE_SIDE
    window = shift_x // step * TILE_SIDE + shift_y // step
    place_of = lax.broadcasted_iota(jnp.int32, (1, width), 1)
    chosen = window == place_of % tile_count
    spread = lax.broadcasted_iota(jnp.int32, (local, width), 1) // tile_count
    spread = (spread == lax.broadcasted_iota(jnp.int32, (local, width), 0)).astype(jnp.float32).astype(jnp.bfloat16)
    for at, part in ((0, first), (width, second)):
        full = jnp.dot(part, spread, preferred_element_type=jnp.float32)
        left_ref[:, at : at + width] = jnp.where(chosen, full, 0.0).astype(jnp.bfloat16)

    if other != strides:
        for at, old in moves:
            mixed_left[at : at + unit, :] = left_ref[old : old + unit, :]

    def left_of(c):
        return left_ref if order(c) == strides else mixed_left

    def res_of(c):
        return res_ref if order(c) == strides else mixed_res

    narrow = min(MATMUL_COLUMNS, wide)

    def multiply(c):
        def tile(i, carry):
            at = pl.ds(pl.multiple_of(c * wide + i * narrow, narrow), narrow)
            acc[:, at] = jnp.dot(left_of(c)[...], s_vmem[:, at], preferred_element_type=jnp.float32)
            return carry

        lax.fori_loop(0, wide // narrow, tile, 0)

    def scatter_rows(c, k):
        size = rows // 2 ** (k + 1)
        base = place(me, order(c), unit, k)
        bit = (me // order(c)[k]) % 2
        keep = pl.ds(pl.multiple_of(base + bit * size, size), size)
        give = pl.ds(pl.multiple_of(base + (1 - bit) * size, size), size)
        slot = pl.ds(rows - 2 * size, size)
        return keep, give, slot

    def start_scatter(c, k):
        _, give, slot = scatter_rows(c, k)
        sbuf[slot, columns(c)] = acc[give, columns(c)].astype(jnp.bfloat16)
        return send(
            sbuf.at[slot, columns(c)],
            rbuf.at[slot, columns(c)],
            send_sem.at[c, k],
            recv_sem.at[c, k],
            partner(order(c)[k]),
        )

    def end_scatter(c, k):
        keep, _, slot = scatter_rows(c, k)
        acc[keep, columns(c)] += rbuf[slot, columns(c)].astype(jnp.float32)

    def residual(c):
        own = mine(levels, order(c))
        scale = jnp.exp2(par_ref[:, 3:4].astype(jnp.float32))
        goal = target_ref[:, columns(c)].astype(jnp.float32) * scale
        res_of(c)[own, columns(c)] = (acc[own, columns(c)] - goal).astype(jnp.bfloat16)

    def start_gather(c, k):
        held = res_of(c).at[mine(k + 1, order(c)), columns(c)]
        at = 2 * levels - 1 - k
        return send(held, held, send_sem.at[c, at], recv_sem.at[c, at], partner(order(c)[k]))

    def slots(c):
        hops = order(c) + order(c)[::-1]
        taken = [0]
        for stride in hops:
            taken.append(taken[-1] + (GAP_NEAR if stride == 1 else GAP_FAR))
        return taken

    flight = {}
    for time in range(CHUNKS + slots(0)[-1]):
        for c in range(CHUNKS):
            if time - c not in slots(c):
                continue
            at = slots(c).index(time - c)
            if at == 0:
                loads[c].wait()
                multiply(c)
            else:
                flight[c].wait_recv()
                if at <= levels:
                    end_scatter(c, at - 1)
            if at < levels:
                flight[c] = start_scatter(c, at)
            elif at < 2 * levels:
                if at == levels:
                    residual(c)
                flight[c] = start_gather(c, 2 * levels - 1 - at)
    for c in range(CHUNKS):
        if order(c) != strides:
            for at, old in moves:
                res_ref[old : old + unit, columns(c)] = mixed_res[at : at + unit, columns(c)]
    for copy in sent:
        copy.wait_send()


def grad_kernel(left_ref, res_ref, out_ref):
    dims = (((0,), (0,)), ((), ()))
    out_ref[...] = lax.dot_general(left_ref[...], res_ref[...], dims, preferred_element_type=jnp.float32).astype(
        out_ref.dtype
    )


def body(n, s_matrix, beam_weight, probe_shift, probe_cutoff, target, target_exp):
    _, local, tile_count, pixels = s_matrix.shape
    probes = probe_shift.shape[0]
    strides, other = orders(n)
    levels = len(strides)
    unit = 2 * probes
    rows = n * unit
    width = local * tile_count
    pars = jnp.concatenate([probe_shift, probe_cutoff[:, None], target_exp[:, None]], axis=1)
    pars = jnp.pad(jnp.concatenate([pars, pars], axis=0), ((0, 0), (0, 124)))
    vmem = pl.BlockSpec(memory_space=pltpu.VMEM)
    res, left = pl.pallas_call(
        functools.partial(wave_kernel, n, local, tile_count, pixels, strides, other),
        out_shape=(
            jax.ShapeDtypeStruct((rows, pixels), jnp.bfloat16),
            jax.ShapeDtypeStruct((rows, 2 * width), jnp.bfloat16),
        ),
        in_specs=[vmem, vmem, vmem, pl.BlockSpec(memory_space=pl.ANY)],
        out_specs=(vmem, vmem),
        scratch_shapes=[
            pltpu.VMEM((rows, 128), jnp.int32),
            pltpu.VMEM((2 * width, pixels), jnp.bfloat16),
            pltpu.VMEM((rows, pixels), jnp.float32),
            pltpu.VMEM((rows, pixels), jnp.bfloat16),
            pltpu.VMEM((rows, pixels), jnp.bfloat16),
            pltpu.VMEM((rows, 2 * width), jnp.bfloat16),
            pltpu.VMEM((rows, pixels), jnp.bfloat16),
            pltpu.SemaphoreType.DMA((n - 1,)),
            pltpu.SemaphoreType.DMA((n - 1,)),
            pltpu.SemaphoreType.DMA((CHUNKS,)),
            pltpu.SemaphoreType.DMA((CHUNKS, 2 * levels)),
            pltpu.SemaphoreType.DMA((CHUNKS, 2 * levels)),
        ],
        compiler_params=pltpu.CompilerParams(
            collective_id=0, has_side_effects=True, vmem_limit_bytes=60 * 2**20
        ),
    )(pars, beam_weight, target.reshape(unit, pixels), s_matrix.reshape(2 * width, pixels))
    tall = min(256, width)
    grad = pl.pallas_call(
        grad_kernel,
        grid=(2 * width // tall,),
        out_shape=jax.ShapeDtypeStruct((2 * width, pixels), jnp.bfloat16),
        in_specs=[
            pl.BlockSpec((rows, tall), lambda i: (0, i)),
            pl.BlockSpec((rows, pixels), lambda i: (0, 0)),
        ],
        out_specs=pl.BlockSpec((tall, pixels), lambda i: (i, 0)),
        compiler_params=pltpu.CompilerParams(vmem_limit_bytes=60 * 2**20),
    )(left, res)
    return grad.reshape(2, local, tile_count, pixels)


def solution(mesh):
    return jax.shard_map(
        functools.partial(body, mesh.shape["beam"]),
        mesh=mesh,
        in_specs=(
            P(None, ("grp", "beam"), None, None),
            P(None, ("grp", "beam")),
            P(("grp", "beam"), None),
            P(("grp", "beam")),
            P(None, ("grp", "beam"), None),
            P(("grp", "beam")),
        ),
        out_specs=P(None, ("grp", "beam"), None, None),
        check_vma=False,
    )
```

```python
import functools
import math

import jax
import jax.numpy as jnp
from jax import lax
from jax.experimental import pallas as pl
from jax.experimental.pallas import tpu as pltpu
from jax.sharding import PartitionSpec as P

SIDE = 32
GRID = 192
TILE_SIDE = 4
TWO_PI = 2.0 * math.pi
CHUNKS = 8
SWAP = True
GAP_NEAR = 2
GAP_FAR = 4
MATMUL_COLUMNS = 512


def stage_strides(n):
    return [2**k for k in range(n.bit_length() - 1)]


def orders(n):
    strides = stage_strides(n)
    other = list(strides)
    if SWAP and len(other) > 2:
        other[1], other[2] = other[2], other[1]
    return strides, other


def place(me, strides, unit, upto):
    levels = len(strides)
    base = 0
    for k in range(upto):
        base = base + (me // strides[k]) % 2 * (unit * 2 ** (levels - 1 - k))
    return base


def wave_kernel(
    n, local, tile_count, pixels, strides, other,
    par_ref, weight_ref, target_ref, s_ref,
    res_ref, left_ref,
    pars, s_vmem, acc, sbuf, rbuf, mixed_left, mixed_res,
    par_send, par_recv, s_sem, send_sem, recv_sem,
):
    levels = len(strides)
    me = lax.axis_index("beam")
    unit = par_ref.shape[0]
    rows = n * unit
    width = local * tile_count
    wide = pixels // CHUNKS

    def order(c):
        return other if c % 2 else strides

    moves = [(place(i, other, unit, levels), place(i, strides, unit, levels)) for i in range(n)]

    def partner(stride):
        return me + (1 - 2 * ((me // stride) % 2)) * stride

    def columns(c):
        return pl.ds(c * wide, wide)

    loads = []
    for c in range(CHUNKS):
        load = pltpu.make_async_copy(s_ref.at[:, columns(c)], s_vmem.at[:, columns(c)], s_sem.at[c])
        load.start()
        loads.append(load)

    barrier = pltpu.get_barrier_semaphore()
    for ahead in range(1, n):
        pl.semaphore_signal(
            barrier, inc=1, device_id={"beam": lax.rem(me + ahead, n)}, device_id_type=pl.DeviceIdType.MESH
        )
    pl.semaphore_wait(barrier, n - 1)

    sent = []

    def send(source, target, send_semaphore, recv_semaphore, peer):
        copy = pltpu.make_async_remote_copy(
            src_ref=source,
            dst_ref=target,
            send_sem=send_semaphore,
            recv_sem=recv_semaphore,
            device_id={"beam": peer},
            device_id_type=pl.DeviceIdType.MESH,
        )
        copy.start()
        sent.append(copy)
        return copy

    def mine(k, steps=strides):
        size = unit * 2 ** (levels - k)
        return pl.ds(pl.multiple_of(place(me, steps, unit, k), size), size)

    pars[mine(levels), :] = par_ref[...]
    asked = [
        send(par_ref, pars.at[mine(levels), :], par_send.at[ahead - 1], par_recv.at[ahead - 1], lax.rem(me + ahead, n))
        for ahead in range(1, n)
    ]
    for copy in asked:
        copy.wait_recv()

    half = SIDE // 2
    beam = me * local + lax.broadcasted_iota(jnp.int32, (1, local), 1)
    freq_x = beam % SIDE - half
    freq_y = beam // SIDE - half
    shift_x = pars[:, 0:1]
    shift_y = pars[:, 1:2]
    cutoff = pars[:, 2:3]
    ramp = (freq_x * shift_x + freq_y * shift_y) % GRID
    phase = ramp.astype(jnp.float32) * (TWO_PI / GRID)
    inside = (freq_x * freq_x + freq_y * freq_y) <= cutoff
    cosine = jnp.cos(phase)
    sine = jnp.sin(phase)
    w_real = weight_ref[0:1, :]
    w_imag = weight_ref[1:2, :]
    c_real = jnp.where(inside, w_real * cosine + w_imag * sine, 0.0)
    c_imag = jnp.where(inside, w_imag * cosine - w_real * sine, 0.0)
    is_real = lax.broadcasted_iota(jnp.int32, (rows, 1), 0) % unit < unit // 2
    first = jnp.where(is_real, c_real, c_imag).astype(jnp.bfloat16)
    second = jnp.where(is_real, -c_imag, c_real).astype(jnp.bfloat16)
    step = GRID // TILE_SIDE
    window = shift_x // step * TILE_SIDE + shift_y // step
    place_of = lax.broadcasted_iota(jnp.int32, (1, width), 1)
    chosen = window == place_of % tile_count
    spread = lax.broadcasted_iota(jnp.int32, (local, width), 1) // tile_count
    spread = (spread == lax.broadcasted_iota(jnp.int32, (local, width), 0)).astype(jnp.float32).astype(jnp.bfloat16)
    for at, part in ((0, first), (width, second)):
        full = jnp.dot(part, spread, preferred_element_type=jnp.float32)
        left_ref[:, at : at + width] = jnp.where(chosen, full, 0.0).astype(jnp.bfloat16)

    if other != strides:
        for at, old in moves:
            mixed_left[at : at + unit, :] = left_ref[old : old + unit, :]

    def left_of(c):
        return left_ref if order(c) == strides else mixed_left

    def res_of(c):
        return res_ref if order(c) == strides else mixed_res

    narrow = min(MATMUL_COLUMNS, wide)

    def multiply(c):
        def tile(i, carry):
            at = pl.ds(pl.multiple_of(c * wide + i * narrow, narrow), narrow)
            acc[:, at] = jnp.dot(left_of(c)[...], s_vmem[:, at], preferred_element_type=jnp.float32)
            return carry

        lax.fori_loop(0, wide // narrow, tile, 0)

    def scatter_rows(c, k):
        size = rows // 2 ** (k + 1)
        base = place(me, order(c), unit, k)
        bit = (me // order(c)[k]) % 2
        keep = pl.ds(pl.multiple_of(base + bit * size, size), size)
        give = pl.ds(pl.multiple_of(base + (1 - bit) * size, size), size)
        slot = pl.ds(rows - 2 * size, size)
        return keep, give, slot

    def start_scatter(c, k):
        _, give, slot = scatter_rows(c, k)
        sbuf[slot, columns(c)] = acc[give, columns(c)].astype(jnp.bfloat16)
        return send(
            sbuf.at[slot, columns(c)],
            rbuf.at[slot, columns(c)],
            send_sem.at[c, k],
            recv_sem.at[c, k],
            partner(order(c)[k]),
        )

    def end_scatter(c, k):
        keep, _, slot = scatter_rows(c, k)
        acc[keep, columns(c)] += rbuf[slot, columns(c)].astype(jnp.float32)

    def residual(c):
        own = mine(levels, order(c))
        scale = jnp.exp2(par_ref[:, 3:4].astype(jnp.float32))
        goal = target_ref[:, columns(c)].astype(jnp.float32) * scale
        res_of(c)[own, columns(c)] = (acc[own, columns(c)] - goal).astype(jnp.bfloat16)

    def start_gather(c, k):
        held = res_of(c).at[mine(k + 1, order(c)), columns(c)]
        at = 2 * levels - 1 - k
        return send(held, held, send_sem.at[c, at], recv_sem.at[c, at], partner(order(c)[k]))

    def slots(c):
        hops = order(c) + order(c)[::-1]
        taken = [0]
        for stride in hops:
            taken.append(taken[-1] + (GAP_NEAR if stride == 1 else GAP_FAR))
        return taken

    flight = {}
    for time in range(CHUNKS + slots(0)[-1]):
        for c in range(CHUNKS):
            if time - c not in slots(c):
                continue
            at = slots(c).index(time - c)
            if at == 0:
                loads[c].wait()
                multiply(c)
            else:
                flight[c].wait_recv()
                if at <= levels:
                    end_scatter(c, at - 1)
            if at < levels:
                flight[c] = start_scatter(c, at)
            elif at < 2 * levels:
                if at == levels:
                    residual(c)
                flight[c] = start_gather(c, 2 * levels - 1 - at)
    for c in range(CHUNKS):
        if order(c) != strides:
            for at, old in moves:
                res_ref[old : old + unit, columns(c)] = mixed_res[at : at + unit, columns(c)]
    for copy in sent:
        copy.wait_send()


def grad_kernel(left_ref, res_ref, out_ref):
    dims = (((0,), (0,)), ((), ()))
    out_ref[...] = lax.dot_general(left_ref[...], res_ref[...], dims, preferred_element_type=jnp.float32).astype(
        out_ref.dtype
    )


def body(n, s_matrix, beam_weight, probe_shift, probe_cutoff, target, target_exp):
    _, local, tile_count, pixels = s_matrix.shape
    probes = probe_shift.shape[0]
    strides, other = orders(n)
    levels = len(strides)
    unit = 2 * probes
    rows = n * unit
    width = local * tile_count
    pars = jnp.concatenate([probe_shift, probe_cutoff[:, None], target_exp[:, None]], axis=1)
    pars = jnp.pad(jnp.concatenate([pars, pars], axis=0), ((0, 0), (0, 124)))
    vmem = pl.BlockSpec(memory_space=pltpu.VMEM)
    res, left = pl.pallas_call(
        functools.partial(wave_kernel, n, local, tile_count, pixels, strides, other),
        out_shape=(
            jax.ShapeDtypeStruct((rows, pixels), jnp.bfloat16),
            jax.ShapeDtypeStruct((rows, 2 * width), jnp.bfloat16),
        ),
        in_specs=[vmem, vmem, vmem, pl.BlockSpec(memory_space=pl.ANY)],
        out_specs=(vmem, vmem),
        scratch_shapes=[
            pltpu.VMEM((rows, 128), jnp.int32),
            pltpu.VMEM((2 * width, pixels), jnp.bfloat16),
            pltpu.VMEM((rows, pixels), jnp.float32),
            pltpu.VMEM((rows, pixels), jnp.bfloat16),
            pltpu.VMEM((rows, pixels), jnp.bfloat16),
            pltpu.VMEM((rows, 2 * width), jnp.bfloat16),
            pltpu.VMEM((rows, pixels), jnp.bfloat16),
            pltpu.SemaphoreType.DMA((n - 1,)),
            pltpu.SemaphoreType.DMA((n - 1,)),
            pltpu.SemaphoreType.DMA((CHUNKS,)),
            pltpu.SemaphoreType.DMA((CHUNKS, 2 * levels)),
            pltpu.SemaphoreType.DMA((CHUNKS, 2 * levels)),
        ],
        compiler_params=pltpu.CompilerParams(
            collective_id=0, has_side_effects=True, vmem_limit_bytes=60 * 2**20
        ),
    )(pars, beam_weight, target.reshape(unit, pixels), s_matrix.reshape(2 * width, pixels))
    tall = min(512, width)
    grad = pl.pallas_call(
        grad_kernel,
        grid=(2 * width // tall,),
        out_shape=jax.ShapeDtypeStruct((2 * width, pixels), jnp.bfloat16),
        in_specs=[
            pl.BlockSpec((rows, tall), lambda i: (0, i)),
            pl.BlockSpec((rows, pixels), lambda i: (0, 0)),
        ],
        out_specs=pl.BlockSpec((tall, pixels), lambda i: (i, 0)),
        compiler_params=pltpu.CompilerParams(vmem_limit_bytes=60 * 2**20),
    )(left, res)
    return grad.reshape(2, local, tile_count, pixels)


def solution(mesh):
    return jax.shard_map(
        functools.partial(body, mesh.shape["beam"]),
        mesh=mesh,
        in_specs=(
            P(None, ("grp", "beam"), None, None),
            P(None, ("grp", "beam")),
            P(("grp", "beam"), None),
            P(("grp", "beam")),
            P(None, ("grp", "beam"), None),
            P(("grp", "beam")),
        ),
        out_specs=P(None, ("grp", "beam"), None, None),
        check_vma=False,
    )
```
